32 devices in a mesh: seq: 8 (over z, core), tp: 4 (over y, x).
Axes of the slice: x: 2, y: 2, z: 4, core: 2. Of those that a mesh axis runs over, the one named last changes fastest.
Arguments:
- q_heads: bfloat16 [1024, 4096], P('seq', 'tp'), may hold values from -200 to 200
- k_heads: bfloat16 [1024, 4096], P('seq', 'tp'), may hold values from -4 to 4
- v_heads: bfloat16 [1024, 4096], P('seq', 'tp'), may hold values from -5 to 5
- grad_attn: bfloat16 [1024, 4096], P('seq', 'tp'), may hold values from -5 to 5
- attn_out: bfloat16 [1024, 4096], P('seq', 'tp'), may hold values from -5 to 5
- gate_q: bfloat16 [1024, 8192], P('seq', 'tp'), may hold values from -5 to 5
- feat_k: bfloat16 [1024, 8192], P('seq', 'tp'), may hold values from -5 to 5
- feat_v: bfloat16 [1024, 8192], P('seq', 'tp'), may hold values from -5 to 5
- conv_out: bfloat16 [1024, 8192], P('seq', 'tp'), may hold values from -5 to 5
- grad_y: bfloat16 [1024, 8192], P('seq', 'tp'), may hold values from -5 to 5
- filters: float32 [64, 128], replicated, may hold values from -0.5 to 0.5
Outputs:
- grad_q: bfloat16 [1024, 4096], P('seq', 'tp')
- grad_k: bfloat16 [1024, 4096], P('seq', 'tp')
- grad_v: bfloat16 [1024, 4096], P('seq', 'tp')
- grad_gate: bfloat16 [1024, 8192], P('seq', 'tp')
- grad_feat_k: bfloat16 [1024, 8192], P('seq', 'tp')
- grad_feat_v: bfloat16 [1024, 8192], P('seq', 'tp')
- grad_filters: float32 [64, 128], replicated
The draws below stay inside these ranges and needn't reach their ends.
All inputs are finite; a program needn't handle non-finite values.
Results may differ from the reference program's by a relative error of at most 0.014.
Values may be sent and summed in bfloat16 or wider, within the bound.
A program may use at most 64 MiB of HBM per device.

```python
import math
import jax
import jax.numpy as jnp
from jax import lax

D = 8192
HEADS = 32
DH = 128
GROUPS = 64
FILT = 128
LENGTH = 1024
TOKENS = 1024


def keys_common(key):
    raw = jax.random.normal(jax.random.fold_in(key, 7), (TOKENS, HEADS * DH), jnp.float32)
    return jnp.clip(raw, -4.0, 4.0)


def draw_k_heads(key, part):
    return keys_common(key).astype(jnp.bfloat16)


def draw_q_heads(key, part):
    base = jnp.clip(jax.random.normal(jax.random.fold_in(key, 8), (TOKENS, HEADS * DH), jnp.float32), -4.0, 4.0)
    return base.astype(jnp.bfloat16)


def steps_of(own_key, dims, shards, low, largest):
    def one(dim, shards_of):
        steps = jax.random.uniform(jax.random.fold_in(jax.random.fold_in(own_key, 6), dim), (shards_of,), jnp.float32, low / len(shards), largest / len(shards))
        return jnp.repeat(jnp.exp(steps), dims[dim] // shards_of).reshape((-1,) + (1,) * (len(dims) - dim - 1))

    level = one(*shards[0])
    for cut in shards[1:]:
        level = level * one(*cut)
    return level


def normal_values(stream_key, extent, spread, bound, shards=(), kind=jnp.bfloat16):
    values = jax.random.normal(stream_key, extent, jnp.float32) * spread
    if len(shards) > 0:
        values = steps_of(stream_key, extent, shards, -0.22, 0.18) * values
    return jnp.clip(values, min=-bound, max=bound).astype(kind)


def setup_inputs(seed: int = 0) -> dict:
    seeds = jax.random.split(jax.random.key(seed), 12)
    q_heads = draw_q_heads(jax.random.fold_in(seeds[11], 71), 0)
    k_heads = draw_k_heads(jax.random.fold_in(seeds[11], 71), 0)
    v_heads = normal_values(seeds[2], (TOKENS, HEADS * DH), 1.0, 5.0, ((0, 8), (1, 4)))
    grad_attn = normal_values(seeds[3], (TOKENS, HEADS * DH), 1.0, 5.0, ((0, 8), (1, 4)))
    attn_out = normal_values(seeds[4], (TOKENS, HEADS * DH), 1.0, 5.0, ((0, 8), (1, 4)))
    gate_q = normal_values(seeds[5], (TOKENS, D), 1.0, 5.0, ((0, 8), (1, 4)))
    feat_k = normal_values(seeds[6], (TOKENS, D), 1.0, 5.0, ((0, 8), (1, 4)))
    feat_v = normal_values(seeds[7], (TOKENS, D), 1.0, 5.0, ((0, 8), (1, 4)))
    conv_out = normal_values(seeds[8], (TOKENS, D), 1.0, 5.0, ((0, 8), (1, 4)))
    grad_y = normal_values(seeds[9], (TOKENS, D), 1.0, 5.0, ((0, 8), (1, 4)))
    filters = normal_values(seeds[10], (GROUPS, FILT), FILT ** -0.5, 0.5, (), jnp.float32)
    return {"q_heads": q_heads, "k_heads": k_heads, "v_heads": v_heads, "grad_attn": grad_attn, "attn_out": attn_out, "gate_q": gate_q, "feat_k": feat_k, "feat_v": feat_v, "conv_out": conv_out, "grad_y": grad_y, "filters": filters}


def wire_split(x):
    high = x.astype(jnp.bfloat16)
    back = lax.optimization_barrier(high).astype(jnp.float32)
    low = (x - back).astype(jnp.bfloat16)
    return back + lax.optimization_barrier(low).astype(jnp.float32)


def head_grads(operands):
    query, keyrow, value, upstream, saved = operands
    scale = 1.0 / (DH ** 0.5)
    scores = jnp.dot(query, keyrow.T, preferred_element_type=jnp.float32) * scale
    causal = jnp.arange(LENGTH)[:, None] >= jnp.arange(LENGTH)[None, :]
    masked = jnp.where(causal, scores, -jnp.inf)
    top = jnp.max(masked, axis=1)
    total = jnp.sum(jnp.where(causal, jnp.exp(scores - top[:, None]), 0.0), axis=1)
    lse = top + jnp.log(total)
    probs = jnp.where(causal, jnp.exp(scores - lse[:, None]), 0.0)
    delta = jnp.sum(upstream.astype(jnp.float32) * saved.astype(jnp.float32), axis=1)
    dprob = jnp.dot(upstream, value.T, preferred_element_type=jnp.float32)
    dscore = probs * (dprob - delta[:, None])
    grad_query = jnp.dot(dscore, keyrow.astype(jnp.float32), precision=lax.Precision.HIGHEST) * scale
    lse_w = wire_split(lse)
    delta_w = wire_split(delta)
    probs_k = jnp.where(causal, jnp.exp(scores - lse_w[:, None]), 0.0)
    dscore_k = probs_k * (dprob - delta_w[:, None])
    grad_value = jnp.dot(probs_k.astype(jnp.bfloat16).T, upstream, preferred_element_type=jnp.float32)
    grad_key = jnp.dot(dscore_k.astype(jnp.bfloat16).T, query, preferred_element_type=jnp.float32) * scale
    return grad_query.astype(jnp.bfloat16), grad_key.astype(jnp.bfloat16), grad_value.astype(jnp.bfloat16)


def split_heads(x):
    return x.reshape(LENGTH, HEADS, DH).transpose(1, 0, 2)


def join_heads(x):
    return x.transpose(1, 0, 2).reshape(TOKENS, HEADS * DH)


def conv_block(operands):
    dz_block, mixed_block, taps_block = operands
    length_fft = 2 * LENGTH
    spectrum_dz = jnp.fft.rfft(dz_block, n=length_fft, axis=0)
    spectrum_taps = jnp.fft.rfft(taps_block, n=length_fft, axis=0)
    spectrum_mixed = jnp.fft.rfft(mixed_block, n=length_fft, axis=0)
    dw_block = jnp.fft.irfft(spectrum_dz * jnp.conj(spectrum_taps), n=length_fft, axis=0)[:LENGTH]
    term_block = jnp.fft.irfft(spectrum_dz * jnp.conj(spectrum_mixed), n=length_fft, axis=0)[:FILT]
    return dw_block.astype(dz_block.dtype), term_block.astype(dz_block.dtype)


def reference(q_heads, k_heads, v_heads, grad_attn, attn_out, gate_q, feat_k, feat_v, conv_out, grad_y, filters):
    grad_query, grad_key, grad_value = lax.map(head_grads, (split_heads(q_heads), split_heads(k_heads), split_heads(v_heads), split_heads(grad_attn), split_heads(attn_out)))
    dz = (grad_y.astype(jnp.float32) * gate_q.astype(jnp.float32)).astype(jnp.bfloat16)
    dz = lax.optimization_barrier(dz).astype(jnp.float32)
    grad_gate = (grad_y.astype(jnp.float32) * conv_out.astype(jnp.float32)).astype(jnp.bfloat16)
    taps = filters[jnp.arange(D) % GROUPS].T
    mixed = feat_k.astype(jnp.float32) * feat_v.astype(jnp.float32)
    block_width = math.gcd(D, 1024)
    blocks = D // block_width

    def to_blocks(x):
        return x.reshape(x.shape[0], blocks, block_width).transpose(1, 0, 2)

    dw_blocks, term_blocks = lax.map(conv_block, (to_blocks(dz), to_blocks(mixed), to_blocks(taps)))
    dw = dw_blocks.transpose(1, 0, 2).reshape(LENGTH, D)
    per_channel = term_blocks.transpose(1, 0, 2).reshape(FILT, D)
    columns = jnp.sum(per_channel.reshape(FILT, D // GROUPS, GROUPS), axis=1)
    norm = 1.0 / ((TOKENS * D / GROUPS) ** 0.5)
    grad_filters = columns.T * norm
    grad_feat_k = (dw * feat_v.astype(jnp.float32)).astype(jnp.bfloat16)
    grad_feat_v = (dw * feat_k.astype(jnp.float32)).astype(jnp.bfloat16)
    return (join_heads(grad_query), join_heads(grad_key), join_heads(grad_value), grad_gate, grad_feat_k, grad_feat_v, grad_filters)
```

```python
import functools

import jax
import jax.numpy as jnp
from jax import lax
from jax.experimental import pallas as pl
from jax.experimental.pallas import tpu as pltpu
from jax.sharding import PartitionSpec as P

HEADS = 32


def from_behind(value, axis, steps):
    count = lax.axis_size(axis)
    leading, last = (max(0, -steps), min(count, count - steps))
    return lax.ppermute(value, axis, [(source, source + steps) for source in range(leading, last)])


def wire_parts(x):
    high = x.astype(jnp.bfloat16)
    back = lax.optimization_barrier(high).astype(jnp.float32)
    low = (x - back).astype(jnp.bfloat16)
    return (high, low)


def local_ring(
    q_heads,
    k_heads,
    v_heads,
    grad_attn,
    attn_out,
    gate_q,
    feat_k,
    feat_v,
    conv_out,
    grad_y,
    filters,
):
    rows = q_heads.shape[0]
    heads_here = HEADS // lax.axis_size("tp")
    width = q_heads.shape[1] // heads_here
    scale = 1.0 / width**0.5
    shards = lax.axis_size("seq")
    place = lax.axis_index("seq")
    queries = q_heads.reshape(rows, heads_here, width)
    upstream = grad_attn.reshape(rows, heads_here, width)
    keys_here = k_heads.reshape(rows, heads_here, width)
    values_here = v_heads.reshape(rows, heads_here, width)
    delta = jnp.sum(
        upstream.astype(jnp.float32)
        * attn_out.reshape(rows, heads_here, width).astype(jnp.float32),
        axis=2,
    )
    delta_heads = delta.T
    diagonal = jnp.arange(rows)[:, None] >= jnp.arange(rows)[None, :]

    def query_tile(state, key_piece, value_piece, live):
        top, total, acc = state
        count = key_piece.shape[0]
        key_block = key_piece.reshape(count, heads_here, width)
        value_block = value_piece.reshape(count, heads_here, width)
        scores = (
            jnp.einsum("qhd,khd->hqk", queries, key_block, preferred_element_type=jnp.float32)
            * scale
        )
        top_new = jnp.maximum(top, jnp.max(jnp.where(live[None], scores, -1e30), axis=2))
        weights = jnp.where(live[None], jnp.exp(scores - top_new[:, :, None]), 0.0)
        decay = jnp.exp(top - top_new)
        dprob = jnp.einsum(
            "qhd,khd->hqk", upstream, value_block, preferred_element_type=jnp.float32
        )
        term = jnp.einsum(
            "hqk,khd->qhd",
            weights * (dprob - delta_heads[:, :, None]),
            key_block.astype(jnp.float32),
            precision=lax.Precision.HIGHEST,
        )
        return (top_new, total * decay + jnp.sum(weights, axis=2), acc * decay.T[:, :, None] + term)

    zero_rows = jnp.zeros((rows, heads_here, width), jnp.float32)
    state = (
        jnp.full((heads_here, rows), -1e30, jnp.float32),
        jnp.zeros((heads_here, rows), jnp.float32),
        zero_rows,
    )
    state = query_tile(state, k_heads, v_heads, diagonal)

    def relay_keys(back, carry):
        inner, moving = carry
        moving = from_behind((moving[0], moving[1]), "seq", 1)
        valid = place >= back
        live = jnp.broadcast_to(valid, (rows, rows))
        inner = query_tile(inner, moving[0], moving[1], live)
        return (inner, moving)

    state, moved = lax.fori_loop(1, shards, relay_keys, (state, (k_heads, v_heads)))
    top, total, acc = state
    lse = (top + jnp.log(total)).T
    grad_query = acc * (1.0 / total).T[:, :, None] * scale
    lse_high, lse_low = wire_parts(lse)
    delta_high, delta_low = wire_parts(delta)
    stats = jnp.stack([lse_high, lse_low, delta_high, delta_low], axis=1)

    def key_tile(inner, query_piece, upstream_piece, stat_piece, live):
        key_grad, value_grad = inner
        count = query_piece.shape[0]
        query_block = query_piece.reshape(count, heads_here, width)
        upstream_block = upstream_piece.reshape(count, heads_here, width)
        lse_w = stat_piece[:, 0].astype(jnp.float32) + stat_piece[:, 1].astype(jnp.float32)
        delta_w = stat_piece[:, 2].astype(jnp.float32) + stat_piece[:, 3].astype(jnp.float32)
        scores = (
            jnp.einsum("qhd,khd->hqk", query_block, keys_here, preferred_element_type=jnp.float32)
            * scale
        )
        probs = jnp.where(live[None], jnp.exp(scores - lse_w.T[:, :, None]), 0.0)
        dprob = jnp.einsum(
            "qhd,khd->hqk", upstream_block, values_here, preferred_element_type=jnp.float32
        )
        dscore = probs * (dprob - delta_w.T[:, :, None])
        value_grad = value_grad + jnp.einsum(
            "hqk,qhd->khd",
            probs.astype(jnp.bfloat16),
            upstream_block,
            preferred_element_type=jnp.float32,
        )
        key_grad = key_grad + jnp.einsum(
            "hqk,qhd->khd",
            dscore.astype(jnp.bfloat16),
            query_block,
            preferred_element_type=jnp.float32,
        )
        return (key_grad, value_grad)

    grads = (zero_rows, zero_rows)
    grads = key_tile(grads, q_heads, grad_attn, stats, diagonal)

    def relay_queries(back, carry):
        inner, moving = carry
        moving = from_behind((moving[0], moving[1], moving[2]), "seq", -1)
        valid = place + back <= shards - 1
        live = jnp.broadcast_to(valid, (rows, rows))
        inner = key_tile(inner, moving[0], moving[1], moving[2], live)
        return (inner, moving)

    grads, moved = lax.fori_loop(1, shards, relay_queries, (grads, (q_heads, grad_attn, stats)))
    key_grad, value_grad = grads
    grad_q = grad_query.astype(jnp.bfloat16).reshape(rows, heads_here * width)
    grad_k = (key_grad * scale).astype(jnp.bfloat16).reshape(rows, heads_here * width)
    grad_v = value_grad.astype(jnp.bfloat16).reshape(rows, heads_here * width)
    span_taps = filters.shape[1]
    groups = filters.shape[0]
    channels = gate_q.shape[1]
    dz = (grad_y.astype(jnp.float32) * gate_q.astype(jnp.float32)).astype(jnp.bfloat16)
    rim = from_behind(dz[: span_taps - 1], "seq", -1)
    grad_gate = (grad_y.astype(jnp.float32) * conv_out.astype(jnp.float32)).astype(jnp.bfloat16)
    padded = jnp.concatenate([dz, rim], axis=0).astype(jnp.float32)
    taps = jnp.tile(filters.T, (1, channels // groups))
    mixed = feat_k.astype(jnp.float32) * feat_v.astype(jnp.float32)
    numbers = ("NWC", "WIO", "NWC")
    dw = lax.conv_general_dilated(
        padded[None],
        taps[:, None, :],
        (1,),
        "VALID",
        dimension_numbers=numbers,
        feature_group_count=channels,
        precision=lax.Precision.HIGHEST,
    )[0]
    local_terms = lax.conv_general_dilated(
        padded[None],
        mixed[:, None, :],
        (1,),
        "VALID",
        dimension_numbers=numbers,
        feature_group_count=channels,
        precision=lax.Precision.HIGHEST,
    )[0]
    grad_feat_k = (dw * feat_v.astype(jnp.float32)).astype(jnp.bfloat16)
    grad_feat_v = (dw * feat_k.astype(jnp.float32)).astype(jnp.bfloat16)
    local_terms = jnp.sum(local_terms.reshape(span_taps, channels // groups, groups), axis=1).T
    filter_total = lax.psum(local_terms, ("seq", "tp"))
    count_all = rows * shards * channels * lax.axis_size("tp") / groups
    grad_filters = filter_total * (1.0 / count_all**0.5)
    return (grad_q, grad_k, grad_v, grad_gate, grad_feat_k, grad_feat_v, grad_filters)


MESH = pl.DeviceIdType.MESH
LANES = 128
LOG2E = 1.4426950408889634


def kernel(
    n,
    tp,
    q_in,
    k_in,
    v_in,
    do_in,
    ao_in,
    gate_in,
    fk_in,
    fv_in,
    co_in,
    gy_in,
    taps,
    gq_out,
    gk_out,
    gv_out,
    gg_out,
    gfk_out,
    gfv_out,
    gf_out,
    heads_q,
    heads_k,
    heads_v,
    heads_do,
    keys_t,
    delta_mine,
    delta_all,
    do_here,
    ao_here,
    gate,
    fk,
    fv,
    co,
    gy,
    dz_here,
    dz_rim,
    dz_all,
    terms,
    partial_mine,
    partial_in,
    across,
    scores,
    acc_k,
    acc_v,
    res_q,
    res_k,
    res_v,
    load_sem,
    own_sem,
    send_in,
    recv_in,
    send_rim,
    recv_rim,
    send_out,
    recv_out,
    own_out,
    send_rs,
    recv_rs,
    send_tp,
    recv_tp,
    send_ag,
    recv_ag,
):
    me = lax.axis_index("seq")
    lane = lax.axis_index("tp")
    rows, width = q_in.shape[0], q_in.shape[1] // n
    channels = gy_in.shape[1]
    span = taps.shape[0]
    scale = 1.0 / width**0.5

    loads = [
        pltpu.make_async_copy(src, dst, load_sem.at[i])
        for i, (src, dst) in enumerate(
            (
                (gy_in, gy),
                (gate_in, gate),
                (do_in, do_here),
                (ao_in, ao_here),
                (fk_in, fk),
                (fv_in, fv),
                (co_in, co),
            )
        )
    ]
    for load in loads:
        load.start()

    barrier = pltpu.get_barrier_semaphore()
    for d in range(1, n):
        pl.semaphore_signal(
            barrier, inc=1, device_id={"seq": lax.rem(me + d, n)}, device_id_type=MESH
        )
    for d in range(1, tp):
        pl.semaphore_signal(
            barrier, inc=1, device_id={"tp": lax.rem(lane + d, tp)}, device_id_type=MESH
        )
    pl.semaphore_wait(barrier, n - 1 + tp - 1)

    def cols(i):
        return pl.ds(pl.multiple_of(i * width, width), width)

    def block(i):
        return pl.ds(pl.multiple_of(i * rows, rows), rows)

    arrays = ((q_in, heads_q), (k_in, heads_k), (v_in, heads_v), (do_in, heads_do))
    sends = []

    def send_array(a):
        src, dst = arrays[a]
        own = pltpu.make_async_copy(src.at[:, cols(me)], dst.at[block(me), :], own_sem.at[a])
        own.start()
        sends.append((own, True))
        for d in range(1, n):
            peer = lax.rem(me + d, n)
            copy = pltpu.make_async_remote_copy(
                src_ref=src.at[:, cols(peer)],
                dst_ref=dst.at[block(me), :],
                send_sem=send_in.at[a, d],
                recv_sem=recv_in.at[a, d],
                device_id={"seq": peer},
                device_id_type=MESH,
            )
            copy.start()
            sends.append((copy, False))

    send_array(0)
    loads[0].wait()
    loads[1].wait()
    tiles = channels // LANES
    for t in range(tiles):
        at = slice(t * LANES, (t + 1) * LANES)
        dz = (gy[:, at].astype(jnp.float32) * gate[:, at].astype(jnp.float32)).astype(jnp.bfloat16)
        dz_here[:, at] = dz
        dz_all[t, 0:rows, :] = dz.astype(jnp.float32)

    def rim_copy():
        return pltpu.make_async_remote_copy(
            src_ref=dz_here,
            dst_ref=dz_rim,
            send_sem=send_rim,
            recv_sem=recv_rim,
            device_id={"seq": lax.rem(me + n - 1, n)},
            device_id_type=MESH,
        )

    @pl.when(me > 0)
    def _():
        rim_copy().start()

    send_array(1)
    send_array(2)
    send_array(3)

    loads[2].wait()
    loads[3].wait()
    for h in range(n):
        at = slice(h * width, (h + 1) * width)
        prod = do_here[:, at].astype(jnp.float32) * ao_here[:, at].astype(jnp.float32)
        line = jnp.sum(prod.T, axis=0, keepdims=True)
        delta_mine[h] = jnp.broadcast_to(line, (8, rows))
    delta_all[me] = delta_mine[me]
    for d in range(1, n):
        peer = lax.rem(me + d, n)
        copy = pltpu.make_async_remote_copy(
            src_ref=delta_mine.at[peer],
            dst_ref=delta_all.at[me],
            send_sem=send_in.at[4, d],
            recv_sem=recv_in.at[4, d],
            device_id={"seq": peer},
            device_id_type=MESH,
        )
        copy.start()
        sends.append((copy, False))

    loads[4].wait()
    loads[5].wait()
    loads[6].wait()
    for t in range(tiles):
        at = slice(t * LANES, (t + 1) * LANES)
        gg_out[:, at] = (gy[:, at].astype(jnp.float32) * co[:, at].astype(jnp.float32)).astype(
            jnp.bfloat16
        )
    terms[...] = jnp.zeros_like(terms)

    @pl.when(me < n - 1)
    def _():
        rim_copy().wait_recv()
        for t in range(tiles):
            at = slice(t * LANES, (t + 1) * LANES)
            dz_all[t, rows : 2 * rows, :] = dz_rim[:, at].astype(jnp.float32)

    @pl.when(me == n - 1)
    def _():
        for t in range(tiles):
            dz_all[t, rows : 2 * rows, :] = jnp.zeros((rows, LANES), jnp.float32)

    def conv_tile(t, carry):
        at = pl.ds(pl.multiple_of(t * LANES, LANES), LANES)
        left = fk[:, at].astype(jnp.float32)
        right = fv[:, at].astype(jnp.float32)
        mixed = left * right

        def tap_step(step, acc):
            base = pl.multiple_of(step * 8, 8)
            for b in range(8):
                x = dz_all[t, pl.ds(base + b, rows), :]
                acc = acc + x * taps[pl.ds(base + b, 1), :]
                folded = jnp.sum((x * mixed).reshape(rows // 8, 8, LANES), axis=0)
                terms[base + b] = terms[base + b] + folded
            return acc

        acc = lax.fori_loop(0, span // 8, tap_step, jnp.zeros((rows, LANES), jnp.float32))
        gfk_out[:, at] = (acc * right).astype(jnp.bfloat16)
        gfv_out[:, at] = (acc * left).astype(jnp.bfloat16)
        return carry

    lax.fori_loop(0, tiles, conv_tile, 0)
    per_lane = jnp.sum(terms[...], axis=1)
    groups = gf_out.shape[0]
    folded = per_lane
    for g in range(1, LANES // groups):
        folded = folded + pltpu.roll(per_lane, g * groups, 1)
    share = groups // n
    partial_mine[...] = folded.T[0:groups, :]

    def slab(i):
        return pl.ds(pl.multiple_of(i * share, share), share)

    partial_in[me] = partial_mine[slab(me), :]
    small = []
    for d in range(1, n):
        peer = lax.rem(me + d, n)
        copy = pltpu.make_async_remote_copy(
            src_ref=partial_mine.at[slab(peer), :],
            dst_ref=partial_in.at[me],
            send_sem=send_rs.at[d],
            recv_sem=recv_rs.at[d],
            device_id={"seq": peer},
            device_id_type=MESH,
        )
        copy.start()
        small.append(copy)

    for copy, is_local in sends:
        if is_local:
            copy.wait()
        else:
            copy.wait_recv()
    for copy in small:
        copy.wait_recv()
    total = partial_in[0]
    for i in range(1, n):
        total = total + partial_in[i]
    across[lane] = total
    crossing = []
    for d in range(1, tp):
        copy = pltpu.make_async_remote_copy(
            src_ref=across.at[lane],
            dst_ref=across.at[lane],
            send_sem=send_tp.at[d],
            recv_sem=recv_tp.at[d],
            device_id={"tp": lax.rem(lane + d, tp)},
            device_id_type=MESH,
        )
        copy.start()
        crossing.append(copy)

    tile = 2 * rows
    steps = n * rows // tile
    for j in range(steps):
        at = slice(j * tile, (j + 1) * tile)
        keys_t[:, at] = heads_k[at, :].T
    acc_k[...] = jnp.zeros_like(acc_k)
    acc_v[...] = jnp.zeros_like(acc_v)
    key_id = lax.broadcasted_iota(jnp.int32, (tile, tile), 0)
    query_id = lax.broadcasted_iota(jnp.int32, (tile, tile), 1)
    nt = (((1,), (1,)), ((), ()))
    nn = (((1,), (0,)), ((), ()))

    def dot(a, b, dims):
        return lax.dot_general(a, b, dims, preferred_element_type=jnp.float32)

    results = ((res_q, gq_out), (res_k, gk_out), (res_v, gv_out))

    def out_copy(a, r, src_rows):
        src, dst = results[a]
        return pltpu.make_async_remote_copy(
            src_ref=src.at[src_rows, :],
            dst_ref=dst.at[:, cols(me)],
            send_sem=send_out.at[a, r],
            recv_sem=recv_out.at[a, me],
            device_id={"seq": r},
            device_id_type=MESH,
        )

    def own_copy(a, r):
        src, dst = results[a]
        return pltpu.make_async_copy(src.at[block(r), :], dst.at[:, cols(me)], own_out.at[a])

    for i in reversed(range(steps)):
        at_q = slice(i * tile, (i + 1) * tile)
        query = heads_q[at_q, :]
        upstream = heads_do[at_q, :]
        delta = jnp.concatenate(
            [delta_all[2 * i][0:1, :], delta_all[2 * i + 1][0:1, :]], axis=1
        )
        top = None
        for j in range(i + 1):
            at_k = slice(j * tile, (j + 1) * tile)
            raw = dot(heads_k[at_k, :], query, nt)
            if j == i:
                raw = jnp.where(key_id <= query_id, raw, -1e30)
            scores[at_k, :] = raw
            high = jnp.max(raw, axis=0, keepdims=True)
            top = high if top is None else jnp.maximum(top, high)
        total = jnp.zeros_like(top)
        for j in range(i + 1):
            at_k = slice(j * tile, (j + 1) * tile)
            weight = jnp.exp2((scores[at_k, :] - top) * (scale * LOG2E))
            scores[at_k, :] = weight
            total = total + jnp.sum(weight, axis=0, keepdims=True)
        lse = top * scale + jnp.log(total)
        lse_high = lse.astype(jnp.bfloat16).astype(jnp.float32)
        lse_w = lse_high + (lse - lse_high).astype(jnp.bfloat16).astype(jnp.float32)
        delta_high = delta.astype(jnp.bfloat16).astype(jnp.float32)
        delta_w = delta_high + (delta - delta_high).astype(jnp.bfloat16).astype(jnp.float32)
        share_q = 1.0 / total
        share_k = share_q * jnp.exp(lse - lse_w)
        grad_t = jnp.zeros((width, tile), jnp.float32)
        for j in range(i + 1):
            at_k = slice(j * tile, (j + 1) * tile)
            weight = scores[at_k, :]
            dprob = dot(heads_v[at_k, :], upstream, nt)
            dscore = (weight * share_q) * (dprob - delta)
            probs_k = weight * share_k
            dscore_k = (probs_k * (dprob - delta_w)).astype(jnp.bfloat16)
            big = dscore.astype(jnp.bfloat16)
            rest = (dscore - big.astype(jnp.float32)).astype(jnp.bfloat16)
            grad_t = grad_t + dot(keys_t[:, at_k], big, nn) + dot(keys_t[:, at_k], rest, nn)
            acc_v[at_k, :] = acc_v[at_k, :] + dot(probs_k.astype(jnp.bfloat16), upstream, nn)
            acc_k[at_k, :] = acc_k[at_k, :] + dot(dscore_k, query, nn)
        res_q[at_q, :] = (grad_t * scale).T.astype(jnp.bfloat16)
        res_k[at_q, :] = (acc_k[at_q, :] * scale).astype(jnp.bfloat16)
        res_v[at_q, :] = acc_v[at_q, :].astype(jnp.bfloat16)
        for r in (2 * i, 2 * i + 1):

            @pl.when(me != r)
            def _():
                for a in range(3):
                    out_copy(a, r, slice(r * rows, (r + 1) * rows)).start()

            @pl.when(me == r)
            def _():
                for a in range(3):
                    own_copy(a, r).start()

    for copy in crossing:
        copy.wait_recv()
    total = across[0]
    for i in range(1, tp):
        total = total + across[i]
    count_all = rows * n * channels * tp / groups
    gf_out[slab(me), :] = total * (1.0 / count_all**0.5)
    gather = []
    for d in range(1, n):
        copy = pltpu.make_async_remote_copy(
            src_ref=gf_out.at[slab(me), :],
            dst_ref=gf_out.at[slab(me), :],
            send_sem=send_ag.at[d],
            recv_sem=recv_ag.at[d],
            device_id={"seq": lax.rem(me + d, n)},
            device_id_type=MESH,
        )
        copy.start()
        gather.append(copy)

    for copy, is_local in sends:
        if not is_local:
            copy.wait_send()
    for copy in small + crossing:
        copy.wait_send()

    @pl.when(me > 0)
    def _():
        rim_copy().wait_send()

    for r in range(n):

        @pl.when(me != r)
        def _():
            for a in range(3):
                out_copy(a, r, slice(r * rows, (r + 1) * rows)).wait_send()

    for a in range(3):
        own_copy(a, me).wait()
        for d in range(1, n):
            peer = lax.rem(me + d, n)
            src, dst = results[a]
            pltpu.make_async_remote_copy(
                src_ref=src.at[block(me), :],
                dst_ref=dst.at[:, cols(peer)],
                send_sem=send_out.at[a, peer],
                recv_sem=recv_out.at[a, peer],
                device_id={"seq": peer},
                device_id_type=MESH,
            ).wait_recv()
    for copy in gather:
        copy.wait()


def local_heads(
    n,
    tp,
    q_heads,
    k_heads,
    v_heads,
    grad_attn,
    attn_out,
    gate_q,
    feat_k,
    feat_v,
    conv_out,
    grad_y,
    filters,
):
    rows, wide = q_heads.shape
    width = wide // n
    channels = gate_q.shape[1]
    groups, span = filters.shape
    taps = jnp.tile(filters.T, (1, LANES // groups))
    share = groups // n
    tiles = channels // LANES
    bf16, f32 = (jnp.bfloat16, jnp.float32)
    anywhere = pl.BlockSpec(memory_space=pl.ANY)
    inside = pl.BlockSpec(memory_space=pltpu.VMEM)
    dma = pltpu.SemaphoreType.DMA
    return pl.pallas_call(
        functools.partial(kernel, n, tp),
        out_shape=(
            [jax.ShapeDtypeStruct((rows, wide), bf16)] * 3
            + [jax.ShapeDtypeStruct((rows, channels), bf16)] * 3
            + [jax.ShapeDtypeStruct((groups, span), f32)]
        ),
        in_specs=[anywhere] * 10 + [inside],
        out_specs=[anywhere] * 3 + [inside] * 4,
        scratch_shapes=(
            [pltpu.VMEM((n * rows, width), bf16)] * 4
            + [
                pltpu.VMEM((width, n * rows), bf16),
                pltpu.VMEM((n, 8, rows), f32),
                pltpu.VMEM((n, 8, rows), f32),
            ]
            + [pltpu.VMEM((rows, wide), bf16)] * 2
            + [pltpu.VMEM((rows, channels), bf16)] * 7
            + [
                pltpu.VMEM((tiles, 2 * rows, LANES), f32),
                pltpu.VMEM((span, 8, LANES), f32),
                pltpu.VMEM((groups, span), f32),
                pltpu.VMEM((n, share, span), f32),
                pltpu.VMEM((tp, share, span), f32),
                pltpu.VMEM((n * rows, 2 * rows), f32),
            ]
            + [pltpu.VMEM((n * rows, width), f32)] * 2
            + [pltpu.VMEM((n * rows, width), bf16)] * 3
            + [
                dma((7,)),
                dma((4,)),
                dma((5, n)),
                dma((5, n)),
                dma,
                dma,
                dma((3, n)),
                dma((3, n)),
                dma((3,)),
                dma((n,)),
                dma((n,)),
                dma((tp,)),
                dma((tp,)),
                dma((n,)),
                dma((n,)),
            ]
        ),
        compiler_params=pltpu.CompilerParams(
            collective_id=0, has_side_effects=True, vmem_limit_bytes=48 * 1024 * 1024
        ),
    )(
        q_heads,
        k_heads,
        v_heads,
        grad_attn,
        attn_out,
        gate_q,
        feat_k,
        feat_v,
        conv_out,
        grad_y,
        taps,
    )


def local(*args):
    n, tp = (lax.axis_size("seq"), lax.axis_size("tp"))
    rows, wide = args[0].shape
    groups, span = args[10].shape
    fits = (
        HEADS // tp == n
        and n > 1
        and tp > 1
        and n % 2 == 0
        and rows == LANES
        and wide == n * LANES
        and span <= rows
        and span == LANES
        and LANES % groups == 0
        and groups % (8 * n) == 0
    )
    if fits:
        return tuple(local_heads(n, tp, *args))
    return local_ring(*args)


def solution(mesh):
    in_specs = (
        P("seq", "tp"),
        P("seq", "tp"),
        P("seq", "tp"),
        P("seq", "tp"),
        P("seq", "tp"),
        P("seq", "tp"),
        P("seq", "tp"),
        P("seq", "tp"),
        P("seq", "tp"),
        P("seq", "tp"),
        P(),
    )
    out_specs = (
        P("seq", "tp"),
        P("seq", "tp"),
        P("seq", "tp"),
        P("seq", "tp"),
        P("seq", "tp"),
        P("seq", "tp"),
        P(),
    )
    return jax.shard_map(local, mesh=mesh, in_specs=in_specs, out_specs=out_specs, check_vma=False)
```

```python
import functools

import jax
import jax.numpy as jnp
from jax import lax
from jax.experimental import pallas as pl
from jax.experimental.pallas import tpu as pltpu
from jax.sharding import PartitionSpec as P

HEADS = 32


def from_behind(value, axis, steps):
    count = lax.axis_size(axis)
    leading, last = (max(0, -steps), min(count, count - steps))
    return lax.ppermute(value, axis, [(source, source + steps) for source in range(leading, last)])


def wire_parts(x):
    high = x.astype(jnp.bfloat16)
    back = lax.optimization_barrier(high).astype(jnp.float32)
    low = (x - back).astype(jnp.bfloat16)
    return (high, low)


def local_ring(
    q_heads,
    k_heads,
    v_heads,
    grad_attn,
    attn_out,
    gate_q,
    feat_k,
    feat_v,
    conv_out,
    grad_y,
    filters,
):
    rows = q_heads.shape[0]
    heads_here = HEADS // lax.axis_size("tp")
    width = q_heads.shape[1] // heads_here
    scale = 1.0 / width**0.5
    shards = lax.axis_size("seq")
    place = lax.axis_index("seq")
    queries = q_heads.reshape(rows, heads_here, width)
    upstream = grad_attn.reshape(rows, heads_here, width)
    keys_here = k_heads.reshape(rows, heads_here, width)
    values_here = v_heads.reshape(rows, heads_here, width)
    delta = jnp.sum(
        upstream.astype(jnp.float32)
        * attn_out.reshape(rows, heads_here, width).astype(jnp.float32),
        axis=2,
    )
    delta_heads = delta.T
    diagonal = jnp.arange(rows)[:, None] >= jnp.arange(rows)[None, :]

    def query_tile(state, key_piece, value_piece, live):
        top, total, acc = state
        count = key_piece.shape[0]
        key_block = key_piece.reshape(count, heads_here, width)
        value_block = value_piece.reshape(count, heads_here, width)
        scores = (
            jnp.einsum("qhd,khd->hqk", queries, key_block, preferred_element_type=jnp.float32)
            * scale
        )
        top_new = jnp.maximum(top, jnp.max(jnp.where(live[None], scores, -1e30), axis=2))
        weights = jnp.where(live[None], jnp.exp(scores - top_new[:, :, None]), 0.0)
        decay = jnp.exp(top - top_new)
        dprob = jnp.einsum(
            "qhd,khd->hqk", upstream, value_block, preferred_element_type=jnp.float32
        )
        term = jnp.einsum(
            "hqk,khd->qhd",
            weights * (dprob - delta_heads[:, :, None]),
            key_block.astype(jnp.float32),
            precision=lax.Precision.HIGHEST,
        )
        return (top_new, total * decay + jnp.sum(weights, axis=2), acc * decay.T[:, :, None] + term)

    zero_rows = jnp.zeros((rows, heads_here, width), jnp.float32)
    state = (
        jnp.full((heads_here, rows), -1e30, jnp.float32),
        jnp.zeros((heads_here, rows), jnp.float32),
        zero_rows,
    )
    state = query_tile(state, k_heads, v_heads, diagonal)

    def relay_keys(back, carry):
        inner, moving = carry
        moving = from_behind((moving[0], moving[1]), "seq", 1)
        valid = place >= back
        live = jnp.broadcast_to(valid, (rows, rows))
        inner = query_tile(inner, moving[0], moving[1], live)
        return (inner, moving)

    state, moved = lax.fori_loop(1, shards, relay_keys, (state, (k_heads, v_heads)))
    top, total, acc = state
    lse = (top + jnp.log(total)).T
    grad_query = acc * (1.0 / total).T[:, :, None] * scale
    lse_high, lse_low = wire_parts(lse)
    delta_high, delta_low = wire_parts(delta)
    stats = jnp.stack([lse_high, lse_low, delta_high, delta_low], axis=1)

    def key_tile(inner, query_piece, upstream_piece, stat_piece, live):
        key_grad, value_grad = inner
        count = query_piece.shape[0]
        query_block = query_piece.reshape(count, heads_here, width)
        upstream_block = upstream_piece.reshape(count, heads_here, width)
        lse_w = stat_piece[:, 0].astype(jnp.float32) + stat_piece[:, 1].astype(jnp.float32)
        delta_w = stat_piece[:, 2].astype(jnp.float32) + stat_piece[:, 3].astype(jnp.float32)
        scores = (
            jnp.einsum("qhd,khd->hqk", query_block, keys_here, preferred_element_type=jnp.float32)
            * scale
        )
        probs = jnp.where(live[None], jnp.exp(scores - lse_w.T[:, :, None]), 0.0)
        dprob = jnp.einsum(
            "qhd,khd->hqk", upstream_block, values_here, preferred_element_type=jnp.float32
        )
        dscore = probs * (dprob - delta_w.T[:, :, None])
        value_grad = value_grad + jnp.einsum(
            "hqk,qhd->khd",
            probs.astype(jnp.bfloat16),
            upstream_block,
            preferred_element_type=jnp.float32,
        )
        key_grad = key_grad + jnp.einsum(
            "hqk,qhd->khd",
            dscore.astype(jnp.bfloat16),
            query_block,
            preferred_element_type=jnp.float32,
        )
        return (key_grad, value_grad)

    grads = (zero_rows, zero_rows)
    grads = key_tile(grads, q_heads, grad_attn, stats, diagonal)

    def relay_queries(back, carry):
        inner, moving = carry
        moving = from_behind((moving[0], moving[1], moving[2]), "seq", -1)
        valid = place + back <= shards - 1
        live = jnp.broadcast_to(valid, (rows, rows))
        inner = key_tile(inner, moving[0], moving[1], moving[2], live)
        return (inner, moving)

    grads, moved = lax.fori_loop(1, shards, relay_queries, (grads, (q_heads, grad_attn, stats)))
    key_grad, value_grad = grads
    grad_q = grad_query.astype(jnp.bfloat16).reshape(rows, heads_here * width)
    grad_k = (key_grad * scale).astype(jnp.bfloat16).reshape(rows, heads_here * width)
    grad_v = value_grad.astype(jnp.bfloat16).reshape(rows, heads_here * width)
    span_taps = filters.shape[1]
    groups = filters.shape[0]
    channels = gate_q.shape[1]
    dz = (grad_y.astype(jnp.float32) * gate_q.astype(jnp.float32)).astype(jnp.bfloat16)
    rim = from_behind(dz[: span_taps - 1], "seq", -1)
    grad_gate = (grad_y.astype(jnp.float32) * conv_out.astype(jnp.float32)).astype(jnp.bfloat16)
    padded = jnp.concatenate([dz, rim], axis=0).astype(jnp.float32)
    taps = jnp.tile(filters.T, (1, channels // groups))
    mixed = feat_k.astype(jnp.float32) * feat_v.astype(jnp.float32)
    numbers = ("NWC", "WIO", "NWC")
    dw = lax.conv_general_dilated(
        padded[None],
        taps[:, None, :],
        (1,),
        "VALID",
        dimension_numbers=numbers,
        feature_group_count=channels,
        precision=lax.Precision.HIGHEST,
    )[0]
    local_terms = lax.conv_general_dilated(
        padded[None],
        mixed[:, None, :],
        (1,),
        "VALID",
        dimension_numbers=numbers,
        feature_group_count=channels,
        precision=lax.Precision.HIGHEST,
    )[0]
    grad_feat_k = (dw * feat_v.astype(jnp.float32)).astype(jnp.bfloat16)
    grad_feat_v = (dw * feat_k.astype(jnp.float32)).astype(jnp.bfloat16)
    local_terms = jnp.sum(local_terms.reshape(span_taps, channels // groups, groups), axis=1).T
    filter_total = lax.psum(local_terms, ("seq", "tp"))
    count_all = rows * shards * channels * lax.axis_size("tp") / groups
    grad_filters = filter_total * (1.0 / count_all**0.5)
    return (grad_q, grad_k, grad_v, grad_gate, grad_feat_k, grad_feat_v, grad_filters)


MESH = pl.DeviceIdType.MESH
LANES = 128
LOG2E = 1.4426950408889634


def kernel(
    n,
    tp,
    q_in,
    k_in,
    v_in,
    do_in,
    ao_in,
    gate_in,
    fk_in,
    fv_in,
    co_in,
    gy_in,
    filters,
    gq_out,
    gk_out,
    gv_out,
    gg_out,
    gfk_out,
    gfv_out,
    gf_out,
    heads_q,
    heads_k,
    heads_v,
    heads_do,
    keys_t,
    delta_mine,
    delta_all,
    do_here,
    ao_here,
    gate,
    fk,
    fv,
    co,
    gy,
    dz_here,
    dz_rim,
    dz_all,
    taps,
    terms,
    partial_mine,
    partial_in,
    across,
    scores,
    acc_k,
    acc_v,
    res_q,
    res_k,
    res_v,
    load_sem,
    own_sem,
    send_in,
    recv_in,
    send_rim,
    recv_rim,
    send_out,
    recv_out,
    own_out,
    send_rs,
    recv_rs,
    send_tp,
    recv_tp,
    send_ag,
    recv_ag,
):
    me = lax.axis_index("seq")
    lane = lax.axis_index("tp")
    rows, width = q_in.shape[0], q_in.shape[1] // n
    channels = gy_in.shape[1]
    span = filters.shape[1]
    scale = 1.0 / width**0.5

    loads = [
        pltpu.make_async_copy(src, dst, load_sem.at[i])
        for i, (src, dst) in enumerate(
            (
                (gy_in, gy),
                (gate_in, gate),
                (do_in, do_here),
                (ao_in, ao_here),
                (fk_in, fk),
                (fv_in, fv),
                (co_in, co),
            )
        )
    ]
    for load in loads:
        load.start()

    barrier = pltpu.get_barrier_semaphore()
    for d in range(1, n):
        pl.semaphore_signal(
            barrier, inc=1, device_id={"seq": lax.rem(me + d, n)}, device_id_type=MESH
        )
    for d in range(1, tp):
        pl.semaphore_signal(
            barrier, inc=1, device_id={"tp": lax.rem(lane + d, tp)}, device_id_type=MESH
        )
    pl.semaphore_wait(barrier, n - 1 + tp - 1)

    def cols(i):
        return pl.ds(pl.multiple_of(i * width, width), width)

    def block(i):
        return pl.ds(pl.multiple_of(i * rows, rows), rows)

    arrays = ((q_in, heads_q), (k_in, heads_k), (v_in, heads_v), (do_in, heads_do))
    sends = []
    for a, (src, dst) in enumerate(arrays):
        own = pltpu.make_async_copy(src.at[:, cols(me)], dst.at[block(me), :], own_sem.at[a])
        own.start()
        sends.append((0, own))
        for d in range(1, n):
            peer = lax.rem(me + d, n)
            copy = pltpu.make_async_remote_copy(
                src_ref=src.at[:, cols(peer)],
                dst_ref=dst.at[block(me), :],
                send_sem=send_in.at[a, d],
                recv_sem=recv_in.at[a, d],
                device_id={"seq": peer},
                device_id_type=MESH,
            )
            sends.append((d, copy))

    def start_sends(later):
        for d, copy in sends:
            if d > 0:

                @pl.when(me + d < n if later else me + d >= n)
                def _():
                    copy.start()

    loads[0].wait()
    loads[1].wait()
    tiles = channels // LANES
    for t in range(tiles):
        at = slice(t * LANES, (t + 1) * LANES)
        dz = (gy[:, at].astype(jnp.float32) * gate[:, at].astype(jnp.float32)).astype(jnp.bfloat16)
        dz_here[:, at] = dz
        dz_all[t, 0:rows, :] = dz.astype(jnp.float32)

    def rim_copy():
        return pltpu.make_async_remote_copy(
            src_ref=dz_here,
            dst_ref=dz_rim,
            send_sem=send_rim,
            recv_sem=recv_rim,
            device_id={"seq": lax.rem(me + n - 1, n)},
            device_id_type=MESH,
        )

    @pl.when(me > 0)
    def _():
        rim_copy().start()

    start_sends(True)

    loads[2].wait()
    loads[3].wait()
    for h in range(n):
        at = slice(h * width, (h + 1) * width)
        prod = do_here[:, at].astype(jnp.float32) * ao_here[:, at].astype(jnp.float32)
        line = jnp.sum(prod.T, axis=0, keepdims=True)
        delta_mine[h] = jnp.broadcast_to(line, (8, rows))
    delta_all[me] = delta_mine[me]
    deltas = []
    for d in range(1, n):
        peer = lax.rem(me + d, n)
        copy = pltpu.make_async_remote_copy(
            src_ref=delta_mine.at[peer],
            dst_ref=delta_all.at[me],
            send_sem=send_in.at[4, d],
            recv_sem=recv_in.at[4, d],
            device_id={"seq": peer},
            device_id_type=MESH,
        )
        copy.start()
        deltas.append(copy)

    loads[4].wait()
    loads[5].wait()
    loads[6].wait()
    for t in range(tiles):
        at = slice(t * LANES, (t + 1) * LANES)
        gg_out[:, at] = (gy[:, at].astype(jnp.float32) * co[:, at].astype(jnp.float32)).astype(
            jnp.bfloat16
        )
    terms[...] = jnp.zeros_like(terms)
    both = jnp.concatenate([filters[...]] * (LANES // filters.shape[0]), axis=0)
    taps[...] = both.T

    @pl.when(me < n - 1)
    def _():
        rim_copy().wait_recv()
        for t in range(tiles):
            at = slice(t * LANES, (t + 1) * LANES)
            dz_all[t, rows : 2 * rows, :] = dz_rim[:, at].astype(jnp.float32)

    @pl.when(me == n - 1)
    def _():
        for t in range(tiles):
            dz_all[t, rows : 2 * rows, :] = jnp.zeros((rows, LANES), jnp.float32)

    @pl.when(me > 0)
    def _():
        rim_copy().wait_send()

    start_sends(False)

    def conv_tile(t, carry):
        at = pl.ds(pl.multiple_of(t * LANES, LANES), LANES)
        left = fk[:, at].astype(jnp.float32)
        right = fv[:, at].astype(jnp.float32)
        mixed = left * right

        def tap_step(step, acc):
            base = pl.multiple_of(step * 8, 8)
            for b in range(8):
                x = dz_all[t, pl.ds(base + b, rows), :]
                acc = acc + x * taps[pl.ds(base + b, 1), :]
                folded = jnp.sum((x * mixed).reshape(rows // 8, 8, LANES), axis=0)
                terms[base + b] = terms[base + b] + folded
            return acc

        acc = lax.fori_loop(0, span // 8, tap_step, jnp.zeros((rows, LANES), jnp.float32))
        gfk_out[:, at] = (acc * right).astype(jnp.bfloat16)
        gfv_out[:, at] = (acc * left).astype(jnp.bfloat16)
        return carry

    lax.fori_loop(0, tiles, conv_tile, 0)
    per_lane = jnp.sum(terms[...], axis=1)
    groups = gf_out.shape[0]
    folded = per_lane
    for g in range(1, LANES // groups):
        folded = folded + pltpu.roll(per_lane, g * groups, 1)
    share = groups // n
    partial_mine[...] = folded.T[0:groups, :]

    def slab(i):
        return pl.ds(pl.multiple_of(i * share, share), share)

    partial_in[me] = partial_mine[slab(me), :]
    small = []
    for d in range(1, n):
        peer = lax.rem(me + d, n)
        copy = pltpu.make_async_remote_copy(
            src_ref=partial_mine.at[slab(peer), :],
            dst_ref=partial_in.at[me],
            send_sem=send_rs.at[d],
            recv_sem=recv_rs.at[d],
            device_id={"seq": peer},
            device_id_type=MESH,
        )
        copy.start()
        small.append(copy)

    for d, copy in sends:
        if d == 0:
            copy.wait()
        else:
            copy.wait_recv()
    for copy in deltas:
        copy.wait_recv()
    for copy in small:
        copy.wait_recv()
    total = partial_in[0]
    for i in range(1, n):
        total = total + partial_in[i]
    across[lane] = total
    crossing = []
    for d in range(1, tp):
        copy = pltpu.make_async_remote_copy(
            src_ref=across.at[lane],
            dst_ref=across.at[lane],
            send_sem=send_tp.at[d],
            recv_sem=recv_tp.at[d],
            device_id={"tp": lax.rem(lane + d, tp)},
            device_id_type=MESH,
        )
        copy.start()
        crossing.append(copy)

    tile = 2 * rows
    steps = n * rows // tile
    for j in range(steps):
        at = slice(j * tile, (j + 1) * tile)
        keys_t[:, at] = heads_k[at, :].T
    acc_k[...] = jnp.zeros_like(acc_k)
    acc_v[...] = jnp.zeros_like(acc_v)
    key_id = lax.broadcasted_iota(jnp.int32, (tile, tile), 0)
    query_id = lax.broadcasted_iota(jnp.int32, (tile, tile), 1)
    nt = (((1,), (1,)), ((), ()))
    nn = (((1,), (0,)), ((), ()))

    def dot(a, b, dims):
        return lax.dot_general(a, b, dims, preferred_element_type=jnp.float32)

    results = ((res_q, gq_out), (res_k, gk_out), (res_v, gv_out))

    def out_copy(a, r, src_rows):
        src, dst = results[a]
        return pltpu.make_async_remote_copy(
            src_ref=src.at[src_rows, :],
            dst_ref=dst.at[:, cols(me)],
            send_sem=send_out.at[a, r],
            recv_sem=recv_out.at[a, me],
            device_id={"seq": r},
            device_id_type=MESH,
        )

    def own_copy(a, r):
        src, dst = results[a]
        return pltpu.make_async_copy(src.at[block(r), :], dst.at[:, cols(me)], own_out.at[a])

    for i in reversed(range(steps)):
        at_q = slice(i * tile, (i + 1) * tile)
        query = heads_q[at_q, :]
        upstream = heads_do[at_q, :]
        delta = jnp.concatenate(
            [delta_all[2 * i][0:1, :], delta_all[2 * i + 1][0:1, :]], axis=1
        )
        top = None
        for j in range(i + 1):
            at_k = slice(j * tile, (j + 1) * tile)
            raw = dot(heads_k[at_k, :], query, nt)
            if j == i:
                raw = jnp.where(key_id <= query_id, raw, -1e30)
            scores[at_k, :] = raw
            high = jnp.max(raw, axis=0, keepdims=True)
            top = high if top is None else jnp.maximum(top, high)
        total = jnp.zeros_like(top)
        for j in range(i + 1):
            at_k = slice(j * tile, (j + 1) * tile)
            weight = jnp.exp2((scores[at_k, :] - top) * (scale * LOG2E))
            scores[at_k, :] = weight
            total = total + jnp.sum(weight, axis=0, keepdims=True)
        lse = top * scale + jnp.log(total)
        lse_high = lse.astype(jnp.bfloat16).astype(jnp.float32)
        lse_w = lse_high + (lse - lse_high).astype(jnp.bfloat16).astype(jnp.float32)
        delta_high = delta.astype(jnp.bfloat16).astype(jnp.float32)
        delta_w = delta_high + (delta - delta_high).astype(jnp.bfloat16).astype(jnp.float32)
        share_q = 1.0 / total
        share_k = share_q * jnp.exp(lse - lse_w)
        grad_t = jnp.zeros((width, tile), jnp.float32)
        for j in range(i + 1):
            at_k = slice(j * tile, (j + 1) * tile)
            weight = scores[at_k, :]
            dprob = dot(heads_v[at_k, :], upstream, nt)
            dscore = (weight * share_q) * (dprob - delta)
            probs_k = weight * share_k
            dscore_k = (probs_k * (dprob - delta_w)).astype(jnp.bfloat16)
            big = dscore.astype(jnp.bfloat16)
            rest = (dscore - big.astype(jnp.float32)).astype(jnp.bfloat16)
            grad_t = grad_t + dot(keys_t[:, at_k], big, nn) + dot(keys_t[:, at_k], rest, nn)
            acc_v[at_k, :] = acc_v[at_k, :] + dot(probs_k.astype(jnp.bfloat16), upstream, nn)
            acc_k[at_k, :] = acc_k[at_k, :] + dot(dscore_k, query, nn)
        res_q[at_q, :] = (grad_t * scale).T.astype(jnp.bfloat16)
        res_k[at_q, :] = (acc_k[at_q, :] * scale).astype(jnp.bfloat16)
        res_v[at_q, :] = acc_v[at_q, :].astype(jnp.bfloat16)
        for r in (2 * i, 2 * i + 1):

            @pl.when(me != r)
            def _():
                for a in range(3):
                    out_copy(a, r, slice(r * rows, (r + 1) * rows)).start()

            @pl.when(me == r)
            def _():
                for a in range(3):
                    own_copy(a, r).start()

    for copy in crossing:
        copy.wait_recv()
    total = across[0]
    for i in range(1, tp):
        total = total + across[i]
    count_all = rows * n * channels * tp / groups
    gf_out[slab(me), :] = total * (1.0 / count_all**0.5)
    gather = []
    for d in range(1, n):
        copy = pltpu.make_async_remote_copy(
            src_ref=gf_out.at[slab(me), :],
            dst_ref=gf_out.at[slab(me), :],
            send_sem=send_ag.at[d],
            recv_sem=recv_ag.at[d],
            device_id={"seq": lax.rem(me + d, n)},
            device_id_type=MESH,
        )
        copy.start()
        gather.append(copy)

    for d, copy in sends:
        if d > 0:
            copy.wait_send()
    for copy in deltas + small + crossing:
        copy.wait_send()

    for r in range(n):

        @pl.when(me != r)
        def _():
            for a in range(3):
                out_copy(a, r, slice(r * rows, (r + 1) * rows)).wait_send()

    for a in range(3):
        own_copy(a, me).wait()
        for d in range(1, n):
            peer = lax.rem(me + d, n)
            src, dst = results[a]
            pltpu.make_async_remote_copy(
                src_ref=src.at[block(me), :],
                dst_ref=dst.at[:, cols(peer)],
                send_sem=send_out.at[a, peer],
                recv_sem=recv_out.at[a, peer],
                device_id={"seq": peer},
                device_id_type=MESH,
            ).wait_recv()
    for copy in gather:
        copy.wait()


def local_heads(
    n,
    tp,
    q_heads,
    k_heads,
    v_heads,
    grad_attn,
    attn_out,
    gate_q,
    feat_k,
    feat_v,
    conv_out,
    grad_y,
    filters,
):
    rows, wide = q_heads.shape
    width = wide // n
    channels = gate_q.shape[1]
    groups, span = filters.shape
    share = groups // n
    tiles = channels // LANES
    bf16, f32 = (jnp.bfloat16, jnp.float32)
    anywhere = pl.BlockSpec(memory_space=pl.ANY)
    inside = pl.BlockSpec(memory_space=pltpu.VMEM)
    dma = pltpu.SemaphoreType.DMA
    return pl.pallas_call(
        functools.partial(kernel, n, tp),
        out_shape=(
            [jax.ShapeDtypeStruct((rows, wide), bf16)] * 3
            + [jax.ShapeDtypeStruct((rows, channels), bf16)] * 3
            + [jax.ShapeDtypeStruct((groups, span), f32)]
        ),
        in_specs=[anywhere] * 10 + [inside],
        out_specs=[anywhere] * 3 + [inside] * 4,
        scratch_shapes=(
            [pltpu.VMEM((n * rows, width), bf16)] * 4
            + [
                pltpu.VMEM((width, n * rows), bf16),
                pltpu.VMEM((n, 8, rows), f32),
                pltpu.VMEM((n, 8, rows), f32),
            ]
            + [pltpu.VMEM((rows, wide), bf16)] * 2
            + [pltpu.VMEM((rows, channels), bf16)] * 7
            + [
                pltpu.VMEM((tiles, 2 * rows, LANES), f32),
                pltpu.VMEM((span, LANES), f32),
                pltpu.VMEM((span, 8, LANES), f32),
                pltpu.VMEM((groups, span), f32),
                pltpu.VMEM((n, share, span), f32),
                pltpu.VMEM((tp, share, span), f32),
                pltpu.VMEM((n * rows, 2 * rows), f32),
            ]
            + [pltpu.VMEM((n * rows, width), f32)] * 2
            + [pltpu.VMEM((n * rows, width), bf16)] * 3
            + [
                dma((7,)),
                dma((4,)),
                dma((5, n)),
                dma((5, n)),
                dma,
                dma,
                dma((3, n)),
                dma((3, n)),
                dma((3,)),
                dma((n,)),
                dma((n,)),
                dma((tp,)),
                dma((tp,)),
                dma((n,)),
                dma((n,)),
            ]
        ),
        compiler_params=pltpu.CompilerParams(
            collective_id=0, has_side_effects=True, vmem_limit_bytes=67043328
        ),
    )(
        q_heads,
        k_heads,
        v_heads,
        grad_attn,
        attn_out,
        gate_q,
        feat_k,
        feat_v,
        conv_out,
        grad_y,
        filters,
    )


def local(*args):
    n, tp = (lax.axis_size("seq"), lax.axis_size("tp"))
    rows, wide = args[0].shape
    groups, span = args[10].shape
    fits = (
        HEADS // tp == n
        and n > 1
        and tp > 1
        and n % 2 == 0
        and rows == LANES
        and wide == n * LANES
        and span <= rows
        and span == LANES
        and LANES % groups == 0
        and groups % (8 * n) == 0
    )
    if fits:
        return tuple(local_heads(n, tp, *args))
    return local_ring(*args)


def solution(mesh):
    in_specs = (
        P("seq", "tp"),
        P("seq", "tp"),
        P("seq", "tp"),
        P("seq", "tp"),
        P("seq", "tp"),
        P("seq", "tp"),
        P("seq", "tp"),
        P("seq", "tp"),
        P("seq", "tp"),
        P("seq", "tp"),
        P(),
    )
    out_specs = (
        P("seq", "tp"),
        P("seq", "tp"),
        P("seq", "tp"),
        P("seq", "tp"),
        P("seq", "tp"),
        P("seq", "tp"),
        P(),
    )
    return jax.shard_map(local, mesh=mesh, in_specs=in_specs, out_specs=out_specs, check_vma=False)
```

```python
import functools

import jax
import jax.numpy as jnp
from jax import lax
from jax.experimental import pallas as pl
from jax.experimental.pallas import tpu as pltpu
from jax.sharding import PartitionSpec as P

HEADS = 32


def from_behind(value, axis, steps):
    count = lax.axis_size(axis)
    leading, last = (max(0, -steps), min(count, count - steps))
    return lax.ppermute(value, axis, [(source, source + steps) for source in range(leading, last)])


def wire_parts(x):
    high = x.astype(jnp.bfloat16)
    back = lax.optimization_barrier(high).astype(jnp.float32)
    low = (x - back).astype(jnp.bfloat16)
    return (high, low)


def local_ring(
    q_heads,
    k_heads,
    v_heads,
    grad_attn,
    attn_out,
    gate_q,
    feat_k,
    feat_v,
    conv_out,
    grad_y,
    filters,
):
    rows = q_heads.shape[0]
    heads_here = HEADS // lax.axis_size("tp")
    width = q_heads.shape[1] // heads_here
    scale = 1.0 / width**0.5
    shards = lax.axis_size("seq")
    place = lax.axis_index("seq")
    queries = q_heads.reshape(rows, heads_here, width)
    upstream = grad_attn.reshape(rows, heads_here, width)
    keys_here = k_heads.reshape(rows, heads_here, width)
    values_here = v_heads.reshape(rows, heads_here, width)
    delta = jnp.sum(
        upstream.astype(jnp.float32)
        * attn_out.reshape(rows, heads_here, width).astype(jnp.float32),
        axis=2,
    )
    delta_heads = delta.T
    diagonal = jnp.arange(rows)[:, None] >= jnp.arange(rows)[None, :]

    def query_tile(state, key_piece, value_piece, live):
        top, total, acc = state
        count = key_piece.shape[0]
        key_block = key_piece.reshape(count, heads_here, width)
        value_block = value_piece.reshape(count, heads_here, width)
        scores = (
            jnp.einsum("qhd,khd->hqk", queries, key_block, preferred_element_type=jnp.float32)
            * scale
        )
        top_new = jnp.maximum(top, jnp.max(jnp.where(live[None], scores, -1e30), axis=2))
        weights = jnp.where(live[None], jnp.exp(scores - top_new[:, :, None]), 0.0)
        decay = jnp.exp(top - top_new)
        dprob = jnp.einsum(
            "qhd,khd->hqk", upstream, value_block, preferred_element_type=jnp.float32
        )
        term = jnp.einsum(
            "hqk,khd->qhd",
            weights * (dprob - delta_heads[:, :, None]),
            key_block.astype(jnp.float32),
            precision=lax.Precision.HIGHEST,
        )
        return (top_new, total * decay + jnp.sum(weights, axis=2), acc * decay.T[:, :, None] + term)

    zero_rows = jnp.zeros((rows, heads_here, width), jnp.float32)
    state = (
        jnp.full((heads_here, rows), -1e30, jnp.float32),
        jnp.zeros((heads_here, rows), jnp.float32),
        zero_rows,
    )
    state = query_tile(state, k_heads, v_heads, diagonal)

    def relay_keys(back, carry):
        inner, moving = carry
        moving = from_behind((moving[0], moving[1]), "seq", 1)
        valid = place >= back
        live = jnp.broadcast_to(valid, (rows, rows))
        inner = query_tile(inner, moving[0], moving[1], live)
        return (inner, moving)

    state, moved = lax.fori_loop(1, shards, relay_keys, (state, (k_heads, v_heads)))
    top, total, acc = state
    lse = (top + jnp.log(total)).T
    grad_query = acc * (1.0 / total).T[:, :, None] * scale
    lse_high, lse_low = wire_parts(lse)
    delta_high, delta_low = wire_parts(delta)
    stats = jnp.stack([lse_high, lse_low, delta_high, delta_low], axis=1)

    def key_tile(inner, query_piece, upstream_piece, stat_piece, live):
        key_grad, value_grad = inner
        count = query_piece.shape[0]
        query_block = query_piece.reshape(count, heads_here, width)
        upstream_block = upstream_piece.reshape(count, heads_here, width)
        lse_w = stat_piece[:, 0].astype(jnp.float32) + stat_piece[:, 1].astype(jnp.float32)
        delta_w = stat_piece[:, 2].astype(jnp.float32) + stat_piece[:, 3].astype(jnp.float32)
        scores = (
            jnp.einsum("qhd,khd->hqk", query_block, keys_here, preferred_element_type=jnp.float32)
            * scale
        )
        probs = jnp.where(live[None], jnp.exp(scores - lse_w.T[:, :, None]), 0.0)
        dprob = jnp.einsum(
            "qhd,khd->hqk", upstream_block, values_here, preferred_element_type=jnp.float32
        )
        dscore = probs * (dprob - delta_w.T[:, :, None])
        value_grad = value_grad + jnp.einsum(
            "hqk,qhd->khd",
            probs.astype(jnp.bfloat16),
            upstream_block,
            preferred_element_type=jnp.float32,
        )
        key_grad = key_grad + jnp.einsum(
            "hqk,qhd->khd",
            dscore.astype(jnp.bfloat16),
            query_block,
            preferred_element_type=jnp.float32,
        )
        return (key_grad, value_grad)

    grads = (zero_rows, zero_rows)
    grads = key_tile(grads, q_heads, grad_attn, stats, diagonal)

    def relay_queries(back, carry):
        inner, moving = carry
        moving = from_behind((moving[0], moving[1], moving[2]), "seq", -1)
        valid = place + back <= shards - 1
        live = jnp.broadcast_to(valid, (rows, rows))
        inner = key_tile(inner, moving[0], moving[1], moving[2], live)
        return (inner, moving)

    grads, moved = lax.fori_loop(1, shards, relay_queries, (grads, (q_heads, grad_attn, stats)))
    key_grad, value_grad = grads
    grad_q = grad_query.astype(jnp.bfloat16).reshape(rows, heads_here * width)
    grad_k = (key_grad * scale).astype(jnp.bfloat16).reshape(rows, heads_here * width)
    grad_v = value_grad.astype(jnp.bfloat16).reshape(rows, heads_here * width)
    span_taps = filters.shape[1]
    groups = filters.shape[0]
    channels = gate_q.shape[1]
    dz = (grad_y.astype(jnp.float32) * gate_q.astype(jnp.float32)).astype(jnp.bfloat16)
    rim = from_behind(dz[: span_taps - 1], "seq", -1)
    grad_gate = (grad_y.astype(jnp.float32) * conv_out.astype(jnp.float32)).astype(jnp.bfloat16)
    padded = jnp.concatenate([dz, rim], axis=0).astype(jnp.float32)
    taps = jnp.tile(filters.T, (1, channels // groups))
    mixed = feat_k.astype(jnp.float32) * feat_v.astype(jnp.float32)
    numbers = ("NWC", "WIO", "NWC")
    dw = lax.conv_general_dilated(
        padded[None],
        taps[:, None, :],
        (1,),
        "VALID",
        dimension_numbers=numbers,
        feature_group_count=channels,
        precision=lax.Precision.HIGHEST,
    )[0]
    local_terms = lax.conv_general_dilated(
        padded[None],
        mixed[:, None, :],
        (1,),
        "VALID",
        dimension_numbers=numbers,
        feature_group_count=channels,
        precision=lax.Precision.HIGHEST,
    )[0]
    grad_feat_k = (dw * feat_v.astype(jnp.float32)).astype(jnp.bfloat16)
    grad_feat_v = (dw * feat_k.astype(jnp.float32)).astype(jnp.bfloat16)
    local_terms = jnp.sum(local_terms.reshape(span_taps, channels // groups, groups), axis=1).T
    filter_total = lax.psum(local_terms, ("seq", "tp"))
    count_all = rows * shards * channels * lax.axis_size("tp") / groups
    grad_filters = filter_total * (1.0 / count_all**0.5)
    return (grad_q, grad_k, grad_v, grad_gate, grad_feat_k, grad_feat_v, grad_filters)


MESH = pl.DeviceIdType.MESH
LANES = 128
LOG2E = 1.4426950408889634


def kernel(
    n,
    tp,
    q_in,
    k_in,
    v_in,
    do_in,
    ao_in,
    gate_in,
    fk_in,
    fv_in,
    co_in,
    gy_in,
    filters,
    gq_out,
    gk_out,
    gv_out,
    gg_out,
    gfk_out,
    gfv_out,
    gf_out,
    heads_q,
    heads_k,
    heads_v,
    heads_do,
    keys_t,
    delta_mine,
    delta_all,
    do_here,
    ao_here,
    gate,
    fk,
    fv,
    co,
    gy,
    dz_here,
    dz_rim,
    dz_all,
    rim_all,
    dw_all,
    taps,
    terms,
    partial_mine,
    partial_in,
    across,
    scores,
    acc_k,
    acc_v,
    res_q,
    res_k,
    res_v,
    load_sem,
    own_sem,
    send_in,
    recv_in,
    send_rim,
    recv_rim,
    send_out,
    recv_out,
    own_out,
    send_rs,
    recv_rs,
    send_tp,
    recv_tp,
    send_ag,
    recv_ag,
):
    me = lax.axis_index("seq")
    lane = lax.axis_index("tp")
    rows, width = q_in.shape[0], q_in.shape[1] // n
    channels = gy_in.shape[1]
    span = filters.shape[1]
    scale = 1.0 / width**0.5

    loads = [
        pltpu.make_async_copy(src, dst, load_sem.at[i])
        for i, (src, dst) in enumerate(
            (
                (gy_in, gy),
                (gate_in, gate),
                (do_in, do_here),
                (ao_in, ao_here),
                (fk_in, fk),
                (fv_in, fv),
                (co_in, co),
            )
        )
    ]
    for load in loads:
        load.start()

    barrier = pltpu.get_barrier_semaphore()
    for d in range(1, n):
        pl.semaphore_signal(
            barrier, inc=1, device_id={"seq": lax.rem(me + d, n)}, device_id_type=MESH
        )
    for d in range(1, tp):
        pl.semaphore_signal(
            barrier, inc=1, device_id={"tp": lax.rem(lane + d, tp)}, device_id_type=MESH
        )
    pl.semaphore_wait(barrier, n - 1 + tp - 1)

    def cols(i):
        return pl.ds(pl.multiple_of(i * width, width), width)

    def block(i):
        return pl.ds(pl.multiple_of(i * rows, rows), rows)

    arrays = ((q_in, heads_q), (k_in, heads_k), (v_in, heads_v), (do_in, heads_do))
    sends = []
    for a, (src, dst) in enumerate(arrays):
        own = pltpu.make_async_copy(src.at[:, cols(me)], dst.at[block(me), :], own_sem.at[a])
        own.start()
        sends.append((0, own))
        for d in range(1, n):
            peer = lax.rem(me + d, n)
            copy = pltpu.make_async_remote_copy(
                src_ref=src.at[:, cols(peer)],
                dst_ref=dst.at[block(me), :],
                send_sem=send_in.at[a, d],
                recv_sem=recv_in.at[a, d],
                device_id={"seq": peer},
                device_id_type=MESH,
            )
            sends.append((d, copy))

    loads[0].wait()
    loads[1].wait()
    tiles = channels // LANES
    for t in range(tiles):
        at = slice(t * LANES, (t + 1) * LANES)
        dz = (gy[:, at].astype(jnp.float32) * gate[:, at].astype(jnp.float32)).astype(jnp.bfloat16)
        dz_here[:, at] = dz
        dz_all[t, 0:rows, :] = dz.astype(jnp.float32)
        dz_all[t, rows : rows + 8, :] = jnp.zeros((8, LANES), jnp.float32)

    def rim_copy():
        return pltpu.make_async_remote_copy(
            src_ref=dz_here,
            dst_ref=dz_rim,
            send_sem=send_rim,
            recv_sem=recv_rim,
            device_id={"seq": lax.rem(me + n - 1, n)},
            device_id_type=MESH,
        )

    @pl.when(me > 0)
    def _():
        rim_copy().start()

    for d, copy in sends:
        if d > 0:
            copy.start()


    loads[2].wait()
    loads[3].wait()
    for h in range(n):
        at = slice(h * width, (h + 1) * width)
        prod = do_here[:, at].astype(jnp.float32) * ao_here[:, at].astype(jnp.float32)
        line = jnp.sum(prod.T, axis=0, keepdims=True)
        delta_mine[h] = jnp.broadcast_to(line, (8, rows))
    delta_all[me] = delta_mine[me]
    deltas = []
    for d in range(1, n):
        peer = lax.rem(me + d, n)
        copy = pltpu.make_async_remote_copy(
            src_ref=delta_mine.at[peer],
            dst_ref=delta_all.at[me],
            send_sem=send_in.at[4, d],
            recv_sem=recv_in.at[4, d],
            device_id={"seq": peer},
            device_id_type=MESH,
        )
        copy.start()
        deltas.append(copy)

    loads[4].wait()
    loads[5].wait()
    loads[6].wait()
    for t in range(tiles):
        at = slice(t * LANES, (t + 1) * LANES)
        gg_out[:, at] = (gy[:, at].astype(jnp.float32) * co[:, at].astype(jnp.float32)).astype(
            jnp.bfloat16
        )
    terms[...] = jnp.zeros_like(terms)
    both = jnp.concatenate([filters[...]] * (LANES // filters.shape[0]), axis=0)
    taps[...] = both.T

    def conv_own(t, carry):
        at = pl.ds(pl.multiple_of(t * LANES, LANES), LANES)
        mixed = fk[:, at].astype(jnp.float32) * fv[:, at].astype(jnp.float32)
        for a in range(span // 8):
            size = rows - 8 * a
            part = None
            for b in range(8):
                tap = 8 * a + b
                x = dz_all[t, tap : tap + size, :]
                term = x * taps[tap : tap + 1, :]
                part = term if part is None else part + term
                prod = (x * mixed[0:size]).reshape(size // 8, 8, LANES)
                terms[tap] = terms[tap] + jnp.sum(prod, axis=0)
            if a == 0:
                dw_all[t] = part
            else:
                dw_all[t, 0:size, :] = dw_all[t, 0:size, :] + part
        return carry

    lax.fori_loop(0, tiles, conv_own, 0)

    for d, copy in sends:
        if d == 0:
            copy.wait()
        else:
            copy.wait_recv()
    for copy in deltas:
        copy.wait_recv()
    tile = 2 * rows
    steps = n * rows // tile
    for j in range(steps):
        at = slice(j * tile, (j + 1) * tile)
        keys_t[:, at] = heads_k[at, :].T
    acc_k[...] = jnp.zeros_like(acc_k)
    acc_v[...] = jnp.zeros_like(acc_v)
    key_id = lax.broadcasted_iota(jnp.int32, (tile, tile), 0)
    query_id = lax.broadcasted_iota(jnp.int32, (tile, tile), 1)
    nt = (((1,), (1,)), ((), ()))
    nn = (((1,), (0,)), ((), ()))

    def dot(a, b, dims):
        return lax.dot_general(a, b, dims, preferred_element_type=jnp.float32)

    results = ((res_q, gq_out), (res_k, gk_out), (res_v, gv_out))

    def out_copy(a, r, src_rows):
        src, dst = results[a]
        return pltpu.make_async_remote_copy(
            src_ref=src.at[src_rows, :],
            dst_ref=dst.at[:, cols(me)],
            send_sem=send_out.at[a, r],
            recv_sem=recv_out.at[a, me],
            device_id={"seq": r},
            device_id_type=MESH,
        )

    def own_copy(a, r):
        src, dst = results[a]
        return pltpu.make_async_copy(src.at[block(r), :], dst.at[:, cols(me)], own_out.at[a])

    for i in reversed(range(steps)):
        at_q = slice(i * tile, (i + 1) * tile)
        query = heads_q[at_q, :]
        upstream = heads_do[at_q, :]
        delta = jnp.concatenate(
            [delta_all[2 * i][0:1, :], delta_all[2 * i + 1][0:1, :]], axis=1
        )
        top = None
        for j in range(i + 1):
            at_k = slice(j * tile, (j + 1) * tile)
            raw = dot(heads_k[at_k, :], query, nt)
            if j == i:
                raw = jnp.where(key_id <= query_id, raw, -1e30)
            scores[at_k, :] = raw
            high = jnp.max(raw, axis=0, keepdims=True)
            top = high if top is None else jnp.maximum(top, high)
        total = jnp.zeros_like(top)
        for j in range(i + 1):
            at_k = slice(j * tile, (j + 1) * tile)
            weight = jnp.exp2((scores[at_k, :] - top) * (scale * LOG2E))
            scores[at_k, :] = weight
            total = total + jnp.sum(weight, axis=0, keepdims=True)
        lse = top * scale + jnp.log(total)
        lse_high = lse.astype(jnp.bfloat16).astype(jnp.float32)
        lse_w = lse_high + (lse - lse_high).astype(jnp.bfloat16).astype(jnp.float32)
        delta_high = delta.astype(jnp.bfloat16).astype(jnp.float32)
        delta_w = delta_high + (delta - delta_high).astype(jnp.bfloat16).astype(jnp.float32)
        share_q = 1.0 / total
        share_k = share_q * jnp.exp(lse - lse_w)
        grad_t = jnp.zeros((width, tile), jnp.float32)
        for j in range(i + 1):
            at_k = slice(j * tile, (j + 1) * tile)
            weight = scores[at_k, :]
            dprob = dot(heads_v[at_k, :], upstream, nt)
            dscore = (weight * share_q) * (dprob - delta)
            probs_k = weight * share_k
            dscore_k = (probs_k * (dprob - delta_w)).astype(jnp.bfloat16)
            big = dscore.astype(jnp.bfloat16)
            rest = (dscore - big.astype(jnp.float32)).astype(jnp.bfloat16)
            grad_t = grad_t + dot(keys_t[:, at_k], big, nn) + dot(keys_t[:, at_k], rest, nn)
            acc_v[at_k, :] = acc_v[at_k, :] + dot(probs_k.astype(jnp.bfloat16), upstream, nn)
            acc_k[at_k, :] = acc_k[at_k, :] + dot(dscore_k, query, nn)
        res_q[at_q, :] = (grad_t * scale).T.astype(jnp.bfloat16)
        res_k[at_q, :] = (acc_k[at_q, :] * scale).astype(jnp.bfloat16)
        res_v[at_q, :] = acc_v[at_q, :].astype(jnp.bfloat16)
        for r in (2 * i, 2 * i + 1):

            @pl.when(me != r)
            def _():
                for a in range(3):
                    out_copy(a, r, slice(r * rows, (r + 1) * rows)).start()

            @pl.when(me == r)
            def _():
                for a in range(3):
                    own_copy(a, r).start()

    @pl.when(me < n - 1)
    def _():
        rim_copy().wait_recv()
        for t in range(tiles):
            at = slice(t * LANES, (t + 1) * LANES)
            rim_all[t, 0:8, :] = jnp.zeros((8, LANES), jnp.float32)
            rim_all[t, 8 : rows + 8, :] = dz_rim[:, at].astype(jnp.float32)

    @pl.when(me == n - 1)
    def _():
        for t in range(tiles):
            rim_all[t, 0 : rows + 8, :] = jnp.zeros((rows + 8, LANES), jnp.float32)

    def conv_rim(t, carry):
        at = pl.ds(pl.multiple_of(t * LANES, LANES), LANES)
        left = fk[:, at].astype(jnp.float32)
        right = fv[:, at].astype(jnp.float32)
        mixed = left * right
        for a in range(span // 8):
            size = 8 * (a + 1)
            part = None
            for b in range(8):
                tap = 8 * a + b
                x = rim_all[t, b : b + size, :]
                term = x * taps[tap : tap + 1, :]
                part = term if part is None else part + term
                prod = (x * mixed[rows - size : rows]).reshape(size // 8, 8, LANES)
                terms[tap] = terms[tap] + jnp.sum(prod, axis=0)
            dw_all[t, rows - size : rows, :] = dw_all[t, rows - size : rows, :] + part
        acc = dw_all[t]
        gfk_out[:, at] = (acc * right).astype(jnp.bfloat16)
        gfv_out[:, at] = (acc * left).astype(jnp.bfloat16)
        return carry

    lax.fori_loop(0, tiles, conv_rim, 0)
    per_lane = jnp.sum(terms[...], axis=1)
    groups = gf_out.shape[0]
    folded = per_lane
    for g in range(1, LANES // groups):
        folded = folded + pltpu.roll(per_lane, g * groups, 1)
    share = groups // n
    partial_mine[...] = folded.T[0:groups, :]

    def slab(i):
        return pl.ds(pl.multiple_of(i * share, share), share)

    partial_in[me] = partial_mine[slab(me), :]
    small = []
    for d in range(1, n):
        peer = lax.rem(me + d, n)
        copy = pltpu.make_async_remote_copy(
            src_ref=partial_mine.at[slab(peer), :],
            dst_ref=partial_in.at[me],
            send_sem=send_rs.at[d],
            recv_sem=recv_rs.at[d],
            device_id={"seq": peer},
            device_id_type=MESH,
        )
        copy.start()
        small.append(copy)

    for copy in small:
        copy.wait_recv()
    total = partial_in[0]
    for i in range(1, n):
        total = total + partial_in[i]
    across[lane] = total
    crossing = []
    for d in range(1, tp):
        copy = pltpu.make_async_remote_copy(
            src_ref=across.at[lane],
            dst_ref=across.at[lane],
            send_sem=send_tp.at[d],
            recv_sem=recv_tp.at[d],
            device_id={"tp": lax.rem(lane + d, tp)},
            device_id_type=MESH,
        )
        copy.start()
        crossing.append(copy)

    for copy in crossing:
        copy.wait_recv()
    total = across[0]
    for i in range(1, tp):
        total = total + across[i]
    count_all = rows * n * channels * tp / groups
    gf_out[slab(me), :] = total * (1.0 / count_all**0.5)
    gather = []
    for d in range(1, n):
        copy = pltpu.make_async_remote_copy(
            src_ref=gf_out.at[slab(me), :],
            dst_ref=gf_out.at[slab(me), :],
            send_sem=send_ag.at[d],
            recv_sem=recv_ag.at[d],
            device_id={"seq": lax.rem(me + d, n)},
            device_id_type=MESH,
        )
        copy.start()
        gather.append(copy)

    @pl.when(me > 0)
    def _():
        rim_copy().wait_send()

    for d, copy in sends:
        if d > 0:
            copy.wait_send()
    for copy in deltas + small + crossing:
        copy.wait_send()

    for r in range(n):

        @pl.when(me != r)
        def _():
            for a in range(3):
                out_copy(a, r, slice(r * rows, (r + 1) * rows)).wait_send()

    for a in range(3):
        own_copy(a, me).wait()
        for d in range(1, n):
            peer = lax.rem(me + d, n)
            src, dst = results[a]
            pltpu.make_async_remote_copy(
                src_ref=src.at[block(me), :],
                dst_ref=dst.at[:, cols(peer)],
                send_sem=send_out.at[a, peer],
                recv_sem=recv_out.at[a, peer],
                device_id={"seq": peer},
                device_id_type=MESH,
            ).wait_recv()
    for copy in gather:
        copy.wait()


def local_heads(
    n,
    tp,
    q_heads,
    k_heads,
    v_heads,
    grad_attn,
    attn_out,
    gate_q,
    feat_k,
    feat_v,
    conv_out,
    grad_y,
    filters,
):
    rows, wide = q_heads.shape
    width = wide // n
    channels = gate_q.shape[1]
    groups, span = filters.shape
    share = groups // n
    tiles = channels // LANES
    bf16, f32 = (jnp.bfloat16, jnp.float32)
    anywhere = pl.BlockSpec(memory_space=pl.ANY)
    inside = pl.BlockSpec(memory_space=pltpu.VMEM)
    dma = pltpu.SemaphoreType.DMA
    return pl.pallas_call(
        functools.partial(kernel, n, tp),
        out_shape=(
            [jax.ShapeDtypeStruct((rows, wide), bf16)] * 3
            + [jax.ShapeDtypeStruct((rows, channels), bf16)] * 3
            + [jax.ShapeDtypeStruct((groups, span), f32)]
        ),
        in_specs=[anywhere] * 10 + [inside],
        out_specs=[anywhere] * 3 + [inside] * 4,
        scratch_shapes=(
            [pltpu.VMEM((n * rows, width), bf16)] * 4
            + [
                pltpu.VMEM((width, n * rows), bf16),
                pltpu.VMEM((n, 8, rows), f32),
                pltpu.VMEM((n, 8, rows), f32),
            ]
            + [pltpu.VMEM((rows, wide), bf16)] * 2
            + [pltpu.VMEM((rows, channels), bf16)] * 7
            + [
                pltpu.VMEM((tiles, rows + 8, LANES), f32),
                pltpu.VMEM((tiles, rows + 16, LANES), f32),
                pltpu.VMEM((tiles, rows, LANES), f32),
                pltpu.VMEM((span, LANES), f32),
                pltpu.VMEM((span, 8, LANES), f32),
                pltpu.VMEM((groups, span), f32),
                pltpu.VMEM((n, share, span), f32),
                pltpu.VMEM((tp, share, span), f32),
                pltpu.VMEM((n * rows, 2 * rows), f32),
            ]
            + [pltpu.VMEM((n * rows, width), f32)] * 2
            + [pltpu.VMEM((n * rows, width), bf16)] * 3
            + [
                dma((7,)),
                dma((4,)),
                dma((5, n)),
                dma((5, n)),
                dma,
                dma,
                dma((3, n)),
                dma((3, n)),
                dma((3,)),
                dma((n,)),
                dma((n,)),
                dma((tp,)),
                dma((tp,)),
                dma((n,)),
                dma((n,)),
            ]
        ),
        compiler_params=pltpu.CompilerParams(
            collective_id=0, has_side_effects=True, vmem_limit_bytes=67043328
        ),
    )(
        q_heads,
        k_heads,
        v_heads,
        grad_attn,
        attn_out,
        gate_q,
        feat_k,
        feat_v,
        conv_out,
        grad_y,
        filters,
    )


def local(*args):
    n, tp = (lax.axis_size("seq"), lax.axis_size("tp"))
    rows, wide = args[0].shape
    groups, span = args[10].shape
    fits = (
        HEADS // tp == n
        and n > 1
        and tp > 1
        and n % 2 == 0
        and rows == LANES
        and wide == n * LANES
        and span <= rows
        and span == LANES
        and LANES % groups == 0
        and groups % (8 * n) == 0
    )
    if fits:
        return tuple(local_heads(n, tp, *args))
    return local_ring(*args)


def solution(mesh):
    in_specs = (
        P("seq", "tp"),
        P("seq", "tp"),
        P("seq", "tp"),
        P("seq", "tp"),
        P("seq", "tp"),
        P("seq", "tp"),
        P("seq", "tp"),
        P("seq", "tp"),
        P("seq", "tp"),
        P("seq", "tp"),
        P(),
    )
    out_specs = (
        P("seq", "tp"),
        P("seq", "tp"),
        P("seq", "tp"),
        P("seq", "tp"),
        P("seq", "tp"),
        P("seq", "tp"),
        P(),
    )
    return jax.shard_map(local, mesh=mesh, in_specs=in_specs, out_specs=out_specs, check_vma=False)
```
